32 devices in a mesh: dp: 8 (over y, x, core), mp: 4 (over z).
Axes of the slice: x: 2, y: 2, z: 4, core: 2. Of those that a mesh axis runs over, the one named last changes fastest.
Arguments:
- tokens: bfloat16 [8192, 2048], P('dp', 'mp'), may hold values from -6 to 6
- segment_ids: int32 [8, 1024], P('dp'), may hold values from 0 to 7, never falling along the last dimension, each value on 1 to 256 neighbouring positions
- w_query: bfloat16 [2048, 2048], P('dp', 'mp'), may hold values from -0.125 to 0.125
- key_matrix: bfloat16 [2048, 1024], P('dp', 'mp'), may hold values from -0.125 to 0.125
- value_matrix: bfloat16 [2048, 1024], P('dp', 'mp'), may hold values from -0.125 to 0.125
- w_out: bfloat16 [2048, 2048], P('mp', 'dp'), may hold values from -1 to 1
- w_gate: bfloat16 [2048, 6144], P('dp', 'mp'), may hold values from -0.125 to 0.125
- w_up: bfloat16 [2048, 6144], P('dp', 'mp'), may hold values from -0.125 to 0.125
- w_down: bfloat16 [6144, 2048], P('mp', 'dp'), may hold values from -0.078125 to 0.078125
- attn_gain: bfloat16 [2048], P('mp'), may hold values from 0.099609375 to 1.8984375
- mlp_gain: bfloat16 [2048], P('mp'), may hold values from 0.099609375 to 1.8984375
- query_gain: bfloat16 [128], replicated, may hold values from 0.099609375 to 1.8984375
- key_gain: bfloat16 [128], replicated, may hold values from 0.099609375 to 1.8984375
- out_grad: bfloat16 [8192, 2048], P('dp', 'mp'), may hold values from -6 to 6
Outputs:
- output: bfloat16 [8192, 2048], P('dp', 'mp')
- grad_input: bfloat16 [8192, 2048], P('dp', 'mp')
- grad_w_query: float32 [2048, 2048], P('dp', 'mp')
- grad_w_key: float32 [2048, 1024], P('dp', 'mp')
- grad_w_value: float32 [2048, 1024], P('dp', 'mp')
- grad_w_out: float32 [2048, 2048], P('mp', 'dp')
- grad_w_gate: float32 [2048, 6144], P('dp', 'mp')
- grad_w_up: float32 [2048, 6144], P('dp', 'mp')
- grad_w_down: float32 [6144, 2048], P('mp', 'dp')
- grad_attn_gain: float32 [2048], P('mp')
- grad_mlp_gain: float32 [2048], P('mp')
- grad_query_gain: float32 [128], replicated
- grad_key_gain: float32 [128], replicated
The draws below stay inside these ranges and needn't reach their ends.
Inputs may be any that keep to these rules, and one draw needn't show every extreme that they name: `segment_ids`: within each packed sequence the ids never fall; every document has 1 to 256 tokens.
All inputs are finite; a program needn't handle non-finite values.
Results may differ from the reference program's by a relative error of at most 0.018.
Values may be sent and summed in bfloat16 or wider, within the bound.
No kernel may reach another device: no remote copies, remote signals or barrier semaphores. Data moves between devices by JAX's collectives and lax.ppermute only.
A program may use at most 256 MiB of HBM per device.

```python
import math
import jax
import jax.numpy as jnp
import numpy as np
from jax import lax

MODEL_WIDTH = 2048
QUERY_HEADS = 16
KEY_VALUE_HEADS = 8
HEAD_WIDTH = 128
FF = 6144
SEQ = 1024
SEGS = 8
SEG_MOST = 256
NSEQ = 8
TOKENS = 8192


def raised(drawn, stream_key, source, target, blocks, factor):
    owner, partner = [(jnp.arange(drawn.shape[position]) // (drawn.shape[position] // blocks)).reshape([-1 if axis == position else 1 for axis in range(drawn.ndim)]) for position in (source, target)]
    chosen = jax.random.permutation(stream_key, blocks)[partner]
    strong = (owner == chosen) | (owner == (partner + blocks // 2) % blocks)
    return jnp.where(strong, factor * drawn, drawn)


def steps_of(rng, dims, split, least, largest):
    level, own = 1.0, jax.random.fold_in(rng, 6)
    for dim, shards_of in split:
        heights = jnp.exp(jax.random.uniform(jax.random.fold_in(own, dim), (shards_of,), jnp.float32, least / len(split), largest / len(split)))
        level = level * jnp.repeat(heights, dims[dim] // shards_of).reshape([-1 if axis == dim else 1 for axis in range(len(dims))])
    return level


def split_up(number_of, total, most, slope):
    weights = [(1 << 20) // math.isqrt(rank ** slope) + 1 for rank in range(2, number_of + 1)]
    rest, holding = total - most - (number_of - 1), [1] * (number_of - 1)
    while rest > 0:
        candidates = [i for i in range(number_of - 1) if holding[i] < most]
        whole, remaining = sum([weights[i] for i in candidates]), rest
        for i in candidates:
            extra = min(most - holding[i], max(1, remaining * weights[i] // whole), rest)
            holding[i] = holding[i] + extra
            rest = rest - extra
    return np.array([most] + holding)


def uneven(key, count, total, reach, skew):
    if count == 2:
        one = jax.random.randint(key, (), max(1, total - reach), min(reach, total - 1) + 1)
        return jnp.stack([one, total - one])
    tallies = jnp.asarray(split_up(count, total, reach, skew), jnp.int32)
    couples = (count - 1) // 2
    giver, sink = tallies[1:1 + 2 * couples:2], tallies[2:2 + 2 * couples:2]
    margin = jnp.minimum(giver - 1, reach - sink)
    passed = jax.random.randint(jax.random.fold_in(key, 1), (couples,), 0, 1 << 20) % (margin + 1)
    tallies = tallies.at[1:1 + 2 * couples:2].set(giver - passed).at[2:2 + 2 * couples:2].set(sink + passed)
    return tallies[jax.random.permutation(jax.random.fold_in(key, 2), count)]


def normal_values(key, dims, scale, reach, pieces=(), held_as=jnp.bfloat16):
    values = scale * jax.random.normal(key, dims, jnp.float32)
    if pieces:
        values = values * steps_of(key, dims, pieces, -0.22, 0.18)
    return jnp.clip(values, -reach, reach).astype(held_as)


def noise_with(rng, dims, scale, limit, shards, heavy, kind=jnp.bfloat16):
    values = scale * jax.random.normal(rng, dims, jnp.float32)
    if shards:
        values = values * steps_of(rng, dims, shards, -0.22, 0.18)
    return jnp.clip(raised(values, jax.random.fold_in(rng, 3), *heavy), -limit, limit).astype(kind)


def setup_inputs(seed: int = 0) -> dict:
    arg_keys = jax.random.split(jax.random.key(seed), 15)
    tokens = noise_with(arg_keys[0], (TOKENS, MODEL_WIDTH), 1.0, 6.0, ((0, 8), (1, 4)), (0, 1, 8, 2.0))
    segment_ids = jax.vmap(lambda own: jnp.searchsorted(jnp.cumsum(uneven(own, SEGS, SEQ, SEG_MOST, 1)), jnp.arange(SEQ), side="right"))(jax.random.split(arg_keys[1], NSEQ)).reshape((NSEQ, SEQ)).astype(jnp.int32)
    w_query = normal_values(arg_keys[2], (MODEL_WIDTH, QUERY_HEADS * HEAD_WIDTH), MODEL_WIDTH ** -0.5, 0.125, ((0, 8), (1, 4)))
    key_matrix = normal_values(arg_keys[3], (MODEL_WIDTH, KEY_VALUE_HEADS * HEAD_WIDTH), MODEL_WIDTH ** -0.5, 0.125, ((0, 8), (1, 4)))
    value_matrix = normal_values(arg_keys[4], (MODEL_WIDTH, KEY_VALUE_HEADS * HEAD_WIDTH), MODEL_WIDTH ** -0.5, 0.125, ((0, 8), (1, 4)))
    w_out = normal_values(arg_keys[5], (QUERY_HEADS * HEAD_WIDTH, MODEL_WIDTH), (QUERY_HEADS * HEAD_WIDTH // 64) ** -0.5, 1.0, ((0, 4), (1, 8)))
    w_gate = normal_values(arg_keys[6], (MODEL_WIDTH, FF), MODEL_WIDTH ** -0.5, 0.125, ((0, 8), (1, 4)))
    w_up = normal_values(arg_keys[7], (MODEL_WIDTH, FF), MODEL_WIDTH ** -0.5, 0.125, ((0, 8), (1, 4)))
    w_down = normal_values(arg_keys[8], (FF, MODEL_WIDTH), FF ** -0.5, 0.078125, ((0, 4), (1, 8)))
    attn_gain = jnp.clip(1.0 + 0.18 * jax.random.normal(arg_keys[9], (MODEL_WIDTH,), jnp.float32), 0.099609375, 1.8984375).astype(jnp.bfloat16)
    mlp_gain = jnp.clip(1.0 + 0.18 * jax.random.normal(arg_keys[10], (MODEL_WIDTH,), jnp.float32), 0.099609375, 1.8984375).astype(jnp.bfloat16)
    query_gain = jnp.clip(1.0 + 0.18 * jax.random.normal(arg_keys[11], (HEAD_WIDTH,), jnp.float32), 0.099609375, 1.8984375).astype(jnp.bfloat16)
    key_gain = jnp.clip(1.0 + 0.18 * jax.random.normal(arg_keys[12], (HEAD_WIDTH,), jnp.float32), 0.099609375, 1.8984375).astype(jnp.bfloat16)
    out_grad = noise_with(arg_keys[13], (TOKENS, MODEL_WIDTH), 1.0, 6.0, ((0, 8), (1, 4)), (0, 1, 8, 2.0))
    return dict(tokens=tokens, segment_ids=segment_ids, w_query=w_query, key_matrix=key_matrix, value_matrix=value_matrix, w_out=w_out, w_gate=w_gate, w_up=w_up, w_down=w_down, attn_gain=attn_gain, mlp_gain=mlp_gain, query_gain=query_gain, key_gain=key_gain, out_grad=out_grad)


EPSILON = 1e-06
ROPE_BASE = 1000000.0
HIGHEST = lax.Precision.HIGHEST

@jax.custom_vjp
def low(v):
    return lax.optimization_barrier(v.astype(jnp.bfloat16)).astype(jnp.float32)

@jax.custom_vjp
def reduced_backward(v):
    return v

def low_keep(v):
    return (low(v), None)

def low_pass(kept, grad):
    return (grad,)

def back_keep(v):
    return (v, None)

def back_low(kept, grad):
    return (low(grad),)
low.defvjp(low_keep, low_pass)
reduced_backward.defvjp(back_keep, back_low)

def matrix_product(left, right):
    return jnp.dot(left, right, precision=HIGHEST, preferred_element_type=jnp.float32)

def row_norm(values, gain):
    inverse = lax.rsqrt(lax.optimization_barrier(jnp.mean(values * values, axis=-1, keepdims=True)) + EPSILON)
    return values * inverse * gain

def positions_of(segments):
    token_length = segments.shape[-1]
    places = jnp.arange(token_length, dtype=jnp.int32)
    change = jnp.concatenate([jnp.ones(segments.shape[:-1] + (1,), jnp.bool_), segments[..., 1:] != segments[..., :-1]], axis=-1)
    starts = jnp.where(change, places, 0).astype(jnp.int32)
    return (places - lax.cummax(starts, axis=segments.ndim - 1)).astype(jnp.int32)

def rope_tables(positions, head_size):
    half_size = head_size // 2
    frequency = ROPE_BASE ** (-(jnp.arange(half_size, dtype=jnp.float32) * 2.0 / head_size))
    angles = positions.astype(jnp.float32)[..., None] * frequency
    return (jnp.cos(angles), jnp.sin(angles))

def rotate(values, cos_table, sin_table):
    half_size = values.shape[-1] // 2
    front_half = values[..., :half_size]
    back_half = values[..., half_size:]
    return jnp.concatenate([front_half * cos_table - back_half * sin_table, back_half * cos_table + front_half * sin_table], axis=-1)

def group_layer(inputs, segments, w_query, key_matrix, value_matrix, w_out, w_gate, w_up, w_down, attn_gain, mlp_gain, query_gain, key_gain):
    local_groups, token_length = segments.shape
    normed_attention = low(row_norm(inputs, attn_gain))
    query_proj = reduced_backward(matrix_product(normed_attention, w_query)).reshape(local_groups, token_length, QUERY_HEADS, HEAD_WIDTH)
    key_projected = reduced_backward(matrix_product(normed_attention, key_matrix)).reshape(local_groups, token_length, KEY_VALUE_HEADS, HEAD_WIDTH)
    value_projected = reduced_backward(matrix_product(normed_attention, value_matrix)).reshape(local_groups, token_length, KEY_VALUE_HEADS, HEAD_WIDTH)
    cos_table, sin_table = rope_tables(positions_of(segments), HEAD_WIDTH)
    cos_heads = cos_table[:, :, None, :]
    sin_heads = sin_table[:, :, None, :]
    query_rot = low(rotate(row_norm(query_proj, query_gain), cos_heads, sin_heads))
    key_rotated = low(rotate(row_norm(key_projected, key_gain), cos_heads, sin_heads))
    value_reduced = low(value_projected)
    key_repeated = jnp.repeat(key_rotated, QUERY_HEADS // KEY_VALUE_HEADS, axis=2)
    value_repeated = jnp.repeat(value_reduced, QUERY_HEADS // KEY_VALUE_HEADS, axis=2)
    scores = reduced_backward(jnp.einsum('gqhd,gkhd->ghqk', query_rot, key_repeated, precision=HIGHEST) * HEAD_WIDTH ** (-0.5))
    places = jnp.arange(token_length, dtype=jnp.int32)
    allowed = (segments[:, :, None] == segments[:, None, :]) & (places[None, :, None] >= places[None, None, :])
    allowed = allowed.astype(jnp.float32)[:, None]
    exp_scores = jnp.exp(scores) * allowed
    probs_low = low(exp_scores / lax.optimization_barrier(jnp.sum(exp_scores, axis=-1, keepdims=True)))
    attended = jnp.einsum('ghqk,gkhd->gqhd', probs_low, value_repeated, precision=HIGHEST)
    attended = low(reduced_backward(attended)).reshape(local_groups * token_length, QUERY_HEADS * HEAD_WIDTH)
    residual = inputs + reduced_backward(matrix_product(attended, w_out))
    normed_mlp = low(row_norm(residual, mlp_gain))
    gate_proj = reduced_backward(matrix_product(normed_mlp, w_gate))
    up_proj = reduced_backward(matrix_product(normed_mlp, w_up))
    hidden_low = low(jax.nn.silu(gate_proj) * up_proj)
    return residual + matrix_product(hidden_low, w_down)

def reference(tokens, segment_ids, w_query, key_matrix, value_matrix, w_out, w_gate, w_up, w_down, attn_gain, mlp_gain, query_gain, key_gain, out_grad):
    per_group = 2 if NSEQ % 2 == 0 else 1
    floats = [array.astype(jnp.float32) for array in (tokens, w_query, key_matrix, value_matrix, w_out, w_gate, w_up, w_down, attn_gain, mlp_gain, query_gain, key_gain)]
    segments = segment_ids.reshape(NSEQ // per_group, per_group, SEQ)

    def forward(inputs, wq_full, wk_full, wv_full, wo_full, wg_full, wu_full, wd_full, gain_attn, gain_mlp, gain_query, gain_key):
        blocks = inputs.reshape(NSEQ // per_group, per_group * SEQ, MODEL_WIDTH)

        def layer_step(paired):
            return group_layer(paired[0], paired[1], wq_full, wk_full, wv_full, wo_full, wg_full, wu_full, wd_full, gain_attn, gain_mlp, gain_query, gain_key)
        result = lax.map(jax.checkpoint(layer_step), (blocks, segments))
        return result.reshape(TOKENS, MODEL_WIDTH)
    result, pullback = jax.vjp(forward, *floats)
    gradients = pullback(out_grad.astype(jnp.float32))
    return (result.astype(jnp.bfloat16), gradients[0].astype(jnp.bfloat16), gradients[1], gradients[2], gradients[3], gradients[4], gradients[5], gradients[6], gradients[7], gradients[8], gradients[9], gradients[10], gradients[11])
```

```python
import functools

import jax
import jax.numpy as jnp
from jax import lax
from jax.experimental import pallas as pl
from jax.experimental.pallas import tpu as pltpu
from jax.sharding import PartitionSpec as P


EPSILON = 1e-06
ROPE_BASE = 1000000.0
DOC_MOST = 256
TILE = 256
HALVES = 2
F32 = jnp.float32
BF16 = jnp.bfloat16
CONTRACT_ROWS = (((0,), (0,)), ((), ()))
CONTRACT_COLS = (((1,), (1,)), ((), ()))


def dot(left, right, dims=(((1,), (0,)), ((), ()))):
    return lax.dot_general(left, right, dims, preferred_element_type=F32)


class Line:
    def __init__(self, size):
        self.size = size
        self.here = lax.axis_index("mp")

    def shard(self, step):
        return lax.rem(self.here - step + self.size, self.size)

    def gather(self, own, axis):
        n = self.size
        up = down = own
        ups, downs = [], []
        for step in range(1, n):
            up = lax.ppermute(up, "mp", [(i, i + 1) for i in range(step - 1, n - 1)])
            down = lax.ppermute(down, "mp", [(i + 1, i) for i in range(0, n - step)])
            ups.append(up)
            downs.append(down)
        shape = list(own.shape)
        width = shape[axis]
        shape[axis] = width * n
        whole = jnp.zeros(shape, own.dtype)

        def put(whole, block, index):
            start = [0] * len(shape)
            start[axis] = index * width
            return lax.dynamic_update_slice(whole, block, start)

        whole = put(whole, own, self.here)
        for step in range(1, n):
            block = jnp.where(self.here >= step, ups[step - 1], downs[n - step - 1])
            whole = put(whole, block, self.shard(step))
        return whole

    def scatter_sum(self, partial, axis):
        n = self.size
        width = partial.shape[axis] // n

        def block(step):
            return lax.dynamic_slice_in_dim(
                partial, self.shard(step) * width, width, axis
            ).astype(F32)

        up = down = None
        for step in range(1, n):
            up_sum, down_sum = block(step), block(n - step)
            if up is not None:
                up_sum = up_sum + up.astype(F32)
                down_sum = down_sum + down.astype(F32)
            up = lax.ppermute(up_sum.astype(BF16), "mp", [(i, i + 1) for i in range(step)])
            down = lax.ppermute(
                down_sum.astype(BF16), "mp", [(i, i - 1) for i in range(n - step, n)]
            )
        total = block(0)
        if up is not None:
            total = total + up.astype(F32) + down.astype(F32)
        return total


def inverse_rms(values):
    return lax.rsqrt(jnp.mean(values * values, axis=-1, keepdims=True) + EPSILON)


def norm_rotate(values, gain, cos_wide, sin_wide):
    normed = values * inverse_rms(values) * gain
    return normed * cos_wide + pltpu.roll(normed, values.shape[-1] // 2, 1) * sin_wide


def norm_rotate_back(grad_rot, values, gain, cos_wide, sin_wide):
    grad_norm = grad_rot * cos_wide - pltpu.roll(grad_rot, values.shape[-1] // 2, 1) * sin_wide
    inverse = inverse_rms(values)
    weighted = grad_norm * gain
    grad = inverse * weighted - values * inverse**3 * jnp.mean(
        weighted * values, axis=-1, keepdims=True
    )
    return grad, jnp.sum(grad_norm * values * inverse, axis=0, keepdims=True)


def allowed_keys(tile, begin):
    rows = begin.shape[0]
    query_at = tile * rows + lax.broadcasted_iota(jnp.int32, (rows, 2 * rows), 0)
    key_at = (tile - 1) * rows + lax.broadcasted_iota(jnp.int32, (rows, 2 * rows), 1)
    return (key_at <= query_at) & (key_at >= begin)


def attend_kernel(
    first_tile, head, group, q_ref, k_ref, v_ref, ke_ref, ve_ref, ki_ref, vi_ref,
    cos_ref, sin_ref, cos_prev, sin_prev, begin_ref, qg_ref, kg_ref, out_ref,
):
    i = pl.program_id(1)
    scale = head**-0.5
    qg, kg = qg_ref[...], kg_ref[...]
    cos, sin = cos_ref[...], sin_ref[...]
    outer = i == 0
    k_prev = jnp.where(outer, ke_ref[...], ki_ref[...])
    v_prev = jnp.where(outer, ve_ref[...], vi_ref[...])
    keys = jnp.concatenate(
        [
            norm_rotate(k_prev, kg, cos_prev[...], sin_prev[...]).astype(BF16),
            norm_rotate(k_ref[...], kg, cos, sin).astype(BF16),
        ],
        axis=0,
    )
    values = jnp.concatenate([v_prev.astype(BF16), v_ref[...].astype(BF16)], axis=0)
    allowed = allowed_keys(first_tile + i, begin_ref[:, :1])
    for h in range(group):
        part = slice(h * head, (h + 1) * head)
        query = norm_rotate(q_ref[:, part], qg, cos, sin).astype(BF16)
        weights = jnp.where(allowed, jnp.exp(dot(query, keys, CONTRACT_COLS) * scale), 0.0)
        probs = (weights / jnp.sum(weights, axis=-1, keepdims=True)).astype(BF16)
        out_ref[:, part] = dot(probs, values).astype(BF16)


def attend(raw, before, part, tables, gains, sizes):
    heads, kv_heads, head = sizes
    group = heads // kv_heads
    rows = raw.shape[0]
    tile = min(TILE, rows)
    tiles = rows // tile
    first = part * tiles
    cos_wide, sin_wide, begin = tables
    k_at, v_at = heads, heads + kv_heads
    last = before.shape[0] // tile - 1

    def prev(i):
        return jnp.maximum(i - 1, 0)

    def table(index):
        return pl.BlockSpec((tile, head), lambda g, i: (index(i), 0))

    own = lambda i: first + i
    ahead = lambda i: jnp.maximum(first + i - 1, 0)
    gain = pl.BlockSpec((1, head), lambda g, i: (0, 0))
    return pl.pallas_call(
        functools.partial(attend_kernel, first, head, group),
        out_shape=jax.ShapeDtypeStruct((rows, heads * head), BF16),
        grid=(kv_heads, tiles),
        in_specs=[
            pl.BlockSpec((tile, group * head), lambda g, i: (i, g)),
            pl.BlockSpec((tile, head), lambda g, i: (i, k_at + g)),
            pl.BlockSpec((tile, head), lambda g, i: (i, v_at + g)),
            pl.BlockSpec((tile, head), lambda g, i: (last, k_at + g)),
            pl.BlockSpec((tile, head), lambda g, i: (last, v_at + g)),
            pl.BlockSpec((tile, head), lambda g, i: (prev(i), k_at + g)),
            pl.BlockSpec((tile, head), lambda g, i: (prev(i), v_at + g)),
            table(own), table(own), table(ahead), table(ahead), table(own), gain, gain,
        ],
        out_specs=pl.BlockSpec((tile, group * head), lambda g, i: (i, g)),
        cost_estimate=pl.CostEstimate(
            flops=8 * rows * tile * heads * head,
            bytes_accessed=rows * 8 * (heads + 2 * kv_heads) * head,
            transcendentals=2 * rows * tile * heads,
        ),
        name="attend",
    )(raw, raw, raw, before, before, raw, raw, cos_wide, sin_wide, cos_wide, sin_wide, begin, *gains)


def attend_back_kernel(
    tiles, head, group, q_ref, k_ref, v_ref, kp_ref, vp_ref, do_ref,
    cos_ref, sin_ref, cos_prev, sin_prev, begin_ref, qg_ref, kg_ref,
    dq_ref, dk_ref, dv_ref, gq_ref, gk_ref, k_own, v_own, k_held, v_held, k_add, v_add,
):
    g, i = pl.program_id(0), pl.program_id(1)
    scale = head**-0.5
    qg, kg = qg_ref[...], kg_ref[...]

    @pl.when((g == 0) & (i == 0))
    def _():
        gq_ref[...] = jnp.zeros_like(gq_ref)
        gk_ref[...] = jnp.zeros_like(gk_ref)

    @pl.when(i < tiles)
    def _():
        cos, sin = cos_ref[...], sin_ref[...]
        keys = jnp.concatenate(
            [
                norm_rotate(kp_ref[...], kg, cos_prev[...], sin_prev[...]).astype(BF16),
                norm_rotate(k_ref[...], kg, cos, sin).astype(BF16),
            ],
            axis=0,
        )
        values = jnp.concatenate([vp_ref[...].astype(BF16), v_ref[...].astype(BF16)], axis=0)
        allowed = allowed_keys(i, begin_ref[:, :1])
        rows = allowed.shape[0]
        grad_keys = jnp.zeros((2 * rows, head), F32)
        grad_values = jnp.zeros((2 * rows, head), F32)
        gain_sum = jnp.zeros((1, head), F32)
        for h in range(group):
            part = slice(h * head, (h + 1) * head)
            raw = q_ref[:, part]
            query = norm_rotate(raw, qg, cos, sin).astype(BF16)
            weights = jnp.where(allowed, jnp.exp(dot(query, keys, CONTRACT_COLS) * scale), 0.0)
            probs = weights / jnp.sum(weights, axis=-1, keepdims=True)
            grad_out = do_ref[:, part]
            grad_probs = dot(grad_out, values, CONTRACT_COLS)
            inner = jnp.sum(probs * grad_probs, axis=-1, keepdims=True)
            grad_scores = (probs * (grad_probs - inner)).astype(BF16)
            grad_query, gain_terms = norm_rotate_back(
                dot(grad_scores, keys) * scale, raw, qg, cos, sin
            )
            dq_ref[:, part] = grad_query.astype(BF16)
            gain_sum = gain_sum + gain_terms
            grad_keys = grad_keys + dot(grad_scores, query, CONTRACT_ROWS)
            grad_values = grad_values + dot(probs.astype(BF16), grad_out, CONTRACT_ROWS)
        gq_ref[...] += gain_sum
        k_add[...], k_own[...] = grad_keys[:rows] * scale, grad_keys[rows:] * scale
        v_add[...], v_own[...] = grad_values[:rows], grad_values[rows:]

    @pl.when(i == tiles)
    def _():
        k_add[...] = jnp.zeros_like(k_add)
        v_add[...] = jnp.zeros_like(v_add)

    @pl.when(i > 0)
    def _():
        grad_key, gain_terms = norm_rotate_back(
            k_held[...] + k_add[...], kp_ref[...], kg, cos_prev[...], sin_prev[...]
        )
        dk_ref[...] = grad_key.astype(BF16)
        dv_ref[...] = (v_held[...] + v_add[...]).astype(BF16)
        gk_ref[...] += gain_terms

    k_held[...] = k_own[...]
    v_held[...] = v_own[...]


def attend_back(raw, grad_attended, tables, gains, sizes):
    heads, kv_heads, head = sizes
    group = heads // kv_heads
    rows = raw.shape[0]
    tile = min(TILE, rows)
    tiles = rows // tile
    cos_wide, sin_wide, begin = tables
    k_at, v_at = heads, heads + kv_heads

    def own(i):
        return jnp.minimum(i, tiles - 1)

    def prev(i):
        return jnp.maximum(i - 1, 0)

    def column(index, at):
        return pl.BlockSpec((tile, head), lambda g, i: (index(i), at + g))

    def table(index):
        return pl.BlockSpec((tile, head), lambda g, i: (index(i), 0))

    wide = pl.BlockSpec((tile, group * head), lambda g, i: (own(i), g))
    gain = pl.BlockSpec((1, head), lambda g, i: (0, 0))
    return pl.pallas_call(
        functools.partial(attend_back_kernel, tiles, head, group),
        out_shape=(
            jax.ShapeDtypeStruct((rows, heads * head), BF16),
            jax.ShapeDtypeStruct((rows, kv_heads * head), BF16),
            jax.ShapeDtypeStruct((rows, kv_heads * head), BF16),
            jax.ShapeDtypeStruct((1, head), F32),
            jax.ShapeDtypeStruct((1, head), F32),
        ),
        grid=(kv_heads, tiles + 1),
        in_specs=[
            wide, column(own, k_at), column(own, v_at), column(prev, k_at), column(prev, v_at), wide,
            table(own), table(own), table(prev), table(prev), table(own), gain, gain,
        ],
        out_specs=(wide, column(prev, 0), column(prev, 0), gain, gain),
        scratch_shapes=[pltpu.VMEM((tile, head), F32)] * 6,
        cost_estimate=pl.CostEstimate(
            flops=20 * rows * tile * heads * head,
            bytes_accessed=rows * 10 * (heads + 2 * kv_heads) * head,
            transcendentals=2 * rows * tile * heads,
        ),
        name="attend_back",
    )(raw, raw, raw, raw, raw, grad_attended, cos_wide, sin_wide, cos_wide, sin_wide, begin, *gains)


def input_grad_kernel(shard, shards, here_ref, d_ref, w_ref, x_ref, gain_ref, add_ref, out_ref, gg_ref):
    t = pl.program_id(0)
    rows, width = x_ref.shape
    inputs = x_ref[...].astype(F32)
    inverse = inverse_rms(inputs)
    grad = dot(d_ref[...], w_ref[...], CONTRACT_COLS)
    normed = inputs * inverse

    @pl.when(t == 0)
    def _():
        gg_ref[...] = jnp.zeros_like(gg_ref)

    gg_ref[...] += jnp.sum(grad * normed, axis=0, keepdims=True)
    weighted = grad * gain_ref[...]
    result = inverse * (weighted - normed * jnp.mean(weighted * normed, axis=-1, keepdims=True))
    for piece in range(rows // shard):
        at = slice(piece * shard, (piece + 1) * shard)
        mine = lax.rem(t * (rows // shard) + piece, shards) == here_ref[0]
        out_ref[at] = (result[at] + jnp.where(mine, add_ref[0], 0.0)).astype(BF16)


def input_grad(here, grads, weights, inputs, gain, added, shards):
    rows, width = inputs.shape
    parts, shard = added.shape[0], added.shape[1]
    tile = min(TILE, rows // parts)
    per_part = rows // parts // tile
    inner = grads.shape[1]
    return pl.pallas_call(
        functools.partial(input_grad_kernel, shard, shards),
        out_shape=(
            jax.ShapeDtypeStruct((rows, width), BF16),
            jax.ShapeDtypeStruct((1, width), F32),
        ),
        grid_spec=pltpu.PrefetchScalarGridSpec(
            num_scalar_prefetch=1,
            grid=(rows // tile,),
            in_specs=[
                pl.BlockSpec((tile, inner), lambda t, z: (t, 0)),
                pl.BlockSpec((width, inner), lambda t, z: (0, 0)),
                pl.BlockSpec((tile, width), lambda t, z: (t, 0)),
                pl.BlockSpec((1, width), lambda t, z: (0, 0)),
                pl.BlockSpec((1, shard, width), lambda t, z: (t // per_part, 0, 0)),
            ],
            out_specs=(
                pl.BlockSpec((tile, width), lambda t, z: (t, 0)),
                pl.BlockSpec((1, width), lambda t, z: (0, 0)),
            ),
        ),
        cost_estimate=pl.CostEstimate(
            flops=2 * rows * width * inner,
            bytes_accessed=2 * (rows * inner + width * inner + 2 * rows * width),
            transcendentals=0,
        ),
        name="input_grad",
    )(here, grads, weights, inputs, gain, added)


def token_tables(segments, head):
    places = jnp.arange(segments.shape[-1], dtype=jnp.int32)
    change = jnp.concatenate([jnp.ones((1,), jnp.bool_), segments[1:] != segments[:-1]])
    begin = lax.cummax(jnp.where(change, places, 0), axis=0)
    lane = jnp.arange(head, dtype=jnp.int32)
    half = head // 2
    frequency = ROPE_BASE ** (-((lane % half).astype(F32) * 2.0 / head))
    angles = (places - begin).astype(F32)[:, None] * frequency
    sign = jnp.where(lane < half, -1.0, 1.0)
    return (
        jnp.cos(angles),
        jnp.sin(angles) * sign,
        jnp.broadcast_to(begin[:, None], (segments.shape[-1], head)),
    )


def gather_dp(weight):
    return lax.all_gather(weight, "dp", axis=0, tiled=True)


def scatter_dp(grad):
    return lax.psum_scatter(grad.astype(BF16), "dp", scatter_dimension=0, tiled=True).astype(F32)


def exchange_sum(values, size):
    distance = 1
    while distance < size:
        values = values + lax.ppermute(values, "dp", [(i, i ^ distance) for i in range(size)])
        distance *= 2
    return values


def on_device(
    dp_size, mp_size, tokens, segment_ids, w_query, key_matrix, value_matrix, w_out, w_gate, w_up,
    w_down, attn_gain, mlp_gain, query_gain, key_gain, out_grad,
):
    line = Line(mp_size)
    here = line.here
    rows, local_width = tokens.shape
    width = local_width * mp_size
    head = query_gain.shape[0]
    heads, kv_heads = w_query.shape[1] // head, key_matrix.shape[1] // head
    sizes = (heads, kv_heads, head)
    part = rows // HALVES
    shard = part // mp_size

    def parts_of(array):
        return [array[h * part : (h + 1) * part] for h in range(HALVES)]

    def my_rows(array):
        return lax.dynamic_slice_in_dim(array, here * shard, shard, 0)

    with jax.named_scope("wg_qkv"):
        w_qkv = gather_dp(jnp.concatenate([w_query, key_matrix, value_matrix], axis=1))
    with jax.named_scope("wg_out"):
        w_o = lax.all_gather(w_out, "dp", axis=1, tiled=True)
    with jax.named_scope("wg_gate"):
        w_g = gather_dp(w_gate)
    with jax.named_scope("wg_up"):
        w_u = gather_dp(w_up)
    with jax.named_scope("wg_down"):
        w_d = lax.all_gather(w_down, "dp", axis=1, tiled=True)

    tables = token_tables(segment_ids[0], head)
    head_gains = (query_gain.astype(F32)[None], key_gain.astype(F32)[None])

    with jax.named_scope("ag_x"):
        sub = 16
        both = jnp.concatenate(
            [attn_gain[None], mlp_gain[None], jnp.zeros((sub - 2, local_width), BF16)], axis=0
        )
        whole = []
        for h, own in enumerate(parts_of(tokens)):
            if h == 0:
                own = jnp.concatenate([own, both], axis=0)
            whole.append(line.gather(own, 1))
        gain_attn = whole[0][part].astype(F32)[None]
        gain_mlp = whole[0][part + 1].astype(F32)[None]
        x_parts = [whole[0][:part]] + whole[1:]

    normed_parts, raw_parts, attended_parts, residuals, normed_mlp = [], [], [], [], []
    for h in range(HALVES):
        with jax.named_scope(f"attn_{h}"):
            inputs = x_parts[h].astype(F32)
            normed = (inputs * inverse_rms(inputs) * gain_attn).astype(BF16)
            raw = dot(normed, w_qkv)
            before = raw_parts[h - 1] if h else raw
            attended = attend(raw, before, h, tables, head_gains, sizes)
            partial = dot(attended, w_o).astype(BF16)
            normed_parts.append(normed)
            raw_parts.append(raw)
            attended_parts.append(attended)
        with jax.named_scope(f"rs_attn_{h}"):
            residual = my_rows(x_parts[h]).astype(F32) + line.scatter_sum(partial, 0)
            residuals.append(residual)
            mine = (residual * inverse_rms(residual) * gain_mlp).astype(BF16)
        with jax.named_scope(f"ag_mlp_{h}"):
            normed_mlp.append(line.gather(mine, 0))

    with jax.named_scope("ag_og"):
        og = line.gather(out_grad, 1)
    og_parts = parts_of(og)

    hiddens, grad_gates, grad_ups, grad_residuals, grad_attn, out_parts = [], [], [], [], [], []
    gain_mlp_grad = jnp.zeros((width,), F32)
    for h in range(HALVES):
        with jax.named_scope(f"mlp_{h}"):
            gate = dot(normed_mlp[h], w_g)
            up = dot(normed_mlp[h], w_u)
            sigmoid = jax.nn.sigmoid(gate)
            silu = gate * sigmoid
            hidden = (silu * up).astype(BF16)
            grad_hidden = dot(og_parts[h], w_d, CONTRACT_COLS)
            grad_gate = (grad_hidden * up * sigmoid * (1.0 + gate * (1.0 - sigmoid))).astype(BF16)
            grad_up = (grad_hidden * silu).astype(BF16)
            partial = (
                dot(grad_gate, w_g, CONTRACT_COLS) + dot(grad_up, w_u, CONTRACT_COLS)
            ).astype(BF16)
            hiddens.append(hidden)
            grad_gates.append(grad_gate)
            grad_ups.append(grad_up)
        with jax.named_scope(f"rs_mlp_{h}"):
            grad_normed = line.scatter_sum(partial, 0)
            residual = residuals[h]
            inverse = inverse_rms(residual)
            weighted = grad_normed * gain_mlp
            normalized = residual * inverse
            grad_residual = my_rows(og_parts[h]).astype(F32) + inverse * (
                weighted - normalized * jnp.mean(weighted * normalized, axis=-1, keepdims=True)
            )
            gain_mlp_grad = gain_mlp_grad + jnp.sum(grad_normed * normalized, axis=0)
            grad_residuals.append(grad_residual)
        with jax.named_scope(f"ag_attn_{h}"):
            grad_attn.append(line.gather(grad_residual.astype(BF16), 0))
        with jax.named_scope(f"down_{h}"):
            own = lax.dynamic_update_slice(
                jnp.zeros((part, width), F32), residuals[h], (here * shard, 0)
            )
            out_parts.append((dot(hidden, w_d) + own).astype(BF16))

    with jax.named_scope("rs_out"):
        output = line.scatter_sum(jnp.concatenate(out_parts, axis=0), 1).astype(BF16)

    with jax.named_scope("wgrad_mlp"):
        hidden = jnp.concatenate(hiddens, axis=0)
        nm = jnp.concatenate(normed_mlp, axis=0)
        grad_w_down = scatter_dp(dot(og, hidden, CONTRACT_ROWS)).T
        grad_w_gate = scatter_dp(dot(nm, jnp.concatenate(grad_gates, axis=0), CONTRACT_ROWS))
        grad_w_up = scatter_dp(dot(nm, jnp.concatenate(grad_ups, axis=0), CONTRACT_ROWS))

    with jax.named_scope("attn_back"):
        ga = jnp.concatenate(grad_attn, axis=0)
        grad_attended = jnp.concatenate(
            [dot(one, w_o, CONTRACT_COLS).astype(BF16) for one in grad_attn], axis=0
        )
        raw = jnp.concatenate(raw_parts, axis=0)
        dq, dk, dv, gq, gk = attend_back(raw, grad_attended, tables, head_gains, sizes)
        d_qkv = jnp.concatenate([dq, dk, dv], axis=1)
        x_full = jnp.concatenate(x_parts, axis=0)
        partial, gain_attn_grad = input_grad(
            here[None].astype(jnp.int32), d_qkv, w_qkv, x_full, gain_attn,
            jnp.stack(grad_residuals), mp_size,
        )
    with jax.named_scope("rs_in"):
        grad_input = line.scatter_sum(partial, 1).astype(BF16)

    with jax.named_scope("wgrad_attn"):
        grad_w_out = scatter_dp(
            dot(ga, jnp.concatenate(attended_parts, axis=0), CONTRACT_ROWS)
        ).T
        grad_qkv = scatter_dp(dot(jnp.concatenate(normed_parts, axis=0), d_qkv, CONTRACT_ROWS))
        q_end, k_end = heads * head, (heads + kv_heads) * head
        grad_w_query, grad_w_key, grad_w_value = (
            grad_qkv[:, :q_end], grad_qkv[:, q_end:k_end], grad_qkv[:, k_end:],
        )

    with jax.named_scope("gains"):
        packed = jnp.concatenate([gain_attn_grad[0], gain_mlp_grad, gq[0], gk[0]]).reshape(-1, head)
        packed = exchange_sum(packed, dp_size)
        total = packed
        up = down = packed
        for step in range(1, mp_size):
            up = lax.ppermute(up, "mp", [(i, i + 1) for i in range(step - 1, mp_size - 1)])
            down = lax.ppermute(down, "mp", [(i + 1, i) for i in range(0, mp_size - step)])
            total = total + up + down
        flat = total.reshape(-1)
        grad_attn_gain = lax.dynamic_slice(flat, (here * local_width,), (local_width,))
        grad_mlp_gain = lax.dynamic_slice(flat, (width + here * local_width,), (local_width,))
        grad_query_gain = flat[2 * width : 2 * width + head]
        grad_key_gain = flat[2 * width + head :]

    return (
        output, grad_input, grad_w_query, grad_w_key, grad_w_value, grad_w_out, grad_w_gate,
        grad_w_up, grad_w_down, grad_attn_gain, grad_mlp_gain, grad_query_gain, grad_key_gain,
    )


def solution(mesh):
    rows_cols, cols_rows = P("dp", "mp"), P("mp", "dp")
    weights = (rows_cols, rows_cols, rows_cols, cols_rows, rows_cols, rows_cols, cols_rows)
    return jax.shard_map(
        functools.partial(on_device, mesh.shape["dp"], mesh.shape["mp"]),
        mesh=mesh,
        in_specs=(rows_cols, P("dp", None), *weights, P("mp"), P("mp"), P(), P(), rows_cols),
        out_specs=(rows_cols, rows_cols, *weights, P("mp"), P("mp"), P(), P()),
        check_vma=False,
    )
```
